256 devices in a mesh: grp: 2 (over z_hi), tok: 16 (over y, z_lo), wid: 8 (over x, core).
Axes of the slice: x: 4, y: 4, z: 8 (z_hi: 2, z_lo: 4; z = z_hi * 4 + z_lo), core: 2. Of those that a mesh axis runs over, the one named last changes fastest.
Arguments:
- inputs: bfloat16 [512, 8192], P(('grp', 'wid'), 'tok'), may hold values from -6 to 6
- parent_gate: bfloat16 [8192, 28672], P('tok', ('grp', 'wid')), may hold values from -0.0625 to 0.0625
- parent_up: bfloat16 [8192, 28672], P('tok', ('grp', 'wid')), may hold values from -0.0625 to 0.0625
- parent_down: bfloat16 [28672, 8192], P(('grp', 'wid'), 'tok'), may hold values from -0.03125 to 0.03125
- first_gate: bfloat16 [8192, 7168], P('tok', ('grp', 'wid')), may hold values from -0.0625 to 0.0625
- first_up: bfloat16 [8192, 7168], P('tok', ('grp', 'wid')), may hold values from -0.0625 to 0.0625
- first_down: bfloat16 [7168, 8192], P(('grp', 'wid'), 'tok'), may hold values from -0.0625 to 0.0625
- second_gate: bfloat16 [8192, 5632], P('tok', ('grp', 'wid')), may hold values from -0.0625 to 0.0625
- second_up: bfloat16 [8192, 5632], P('tok', ('grp', 'wid')), may hold values from -0.0625 to 0.0625
- second_down: bfloat16 [5632, 8192], P(('grp', 'wid'), 'tok'), may hold values from -0.078125 to 0.078125
Outputs:
- target: bfloat16 [512, 8192], P(('grp', 'wid'), 'tok')
- first_error: bfloat16 [512, 8192], P(('grp', 'wid'), 'tok')
- second_error: bfloat16 [512, 8192], P(('grp', 'wid'), 'tok')
- first_grad_gate: bfloat16 [8192, 7168], P('tok', ('grp', 'wid'))
- first_grad_up: bfloat16 [8192, 7168], P('tok', ('grp', 'wid'))
- first_grad_down: bfloat16 [7168, 8192], P(('grp', 'wid'), 'tok')
- second_grad_gate: bfloat16 [8192, 5632], P('tok', ('grp', 'wid'))
- second_grad_up: bfloat16 [8192, 5632], P('tok', ('grp', 'wid'))
- second_grad_down: bfloat16 [5632, 8192], P(('grp', 'wid'), 'tok')
The draws below stay inside these ranges and needn't reach their ends.
All inputs are finite; a program needn't handle non-finite values.
Results may differ from the reference program's by a relative error of at most 0.009.
Values may be sent and summed in bfloat16 or wider, within the bound.
No kernel may reach another device: no remote copies, remote signals or barrier semaphores. Data moves between devices by JAX's collectives and lax.ppermute only.
A program may use at most 128 MiB of HBM per device.

```python
import jax
import jax.numpy as jnp
from jax import lax

D = 8192
FF = 28672
HA = 7168
HB = 5632
TOKENS = 512


def level_of(rng, extent, shards, low, top_value):
    factor_of = 1.0
    for axis_at, shards_of in shards:
        steps = jax.random.uniform(jax.random.fold_in(jax.random.fold_in(rng, 6), axis_at), (shards_of,), jnp.float32, low / len(shards), top_value / len(shards))
        factor_of = factor_of * jnp.repeat(jnp.exp(steps), extent[axis_at] // shards_of).reshape((-1,) + (1,) * (len(extent) - 1 - axis_at))
    return factor_of


def normal_values(own_key, extent, width, limit, pieces=(), kind=jnp.bfloat16):
    drawn = jax.random.normal(own_key, extent, jnp.float32) * width
    if len(pieces) > 0:
        drawn = level_of(own_key, extent, pieces, -0.22, 0.18) * drawn
    return jnp.clip(drawn, min=-limit, max=limit).astype(kind)


def setup_inputs(seed: int = 0) -> dict:
    arg_keys = jax.random.split(jax.random.key(seed), 11)
    inputs = normal_values(arg_keys[0], (TOKENS, D), 1.0, 6.0, ((0, 16), (1, 16)))
    parent_gate = normal_values(arg_keys[1], (D, FF), D ** -0.5, 0.0625, ((0, 16), (1, 16)))
    parent_up = normal_values(arg_keys[2], (D, FF), D ** -0.5, 0.0625, ((0, 16), (1, 16)))
    parent_down = normal_values(arg_keys[3], (FF, D), FF ** -0.5, 0.03125, ((0, 16), (1, 16)))
    first_gate = normal_values(arg_keys[4], (D, HA), D ** -0.5, 0.0625, ((0, 16), (1, 16)))
    first_up = normal_values(arg_keys[5], (D, HA), D ** -0.5, 0.0625, ((0, 16), (1, 16)))
    first_down = normal_values(arg_keys[6], (HA, D), HA ** -0.5, 0.0625, ((0, 16), (1, 16)))
    second_gate = normal_values(arg_keys[7], (D, HB), D ** -0.5, 0.0625, ((0, 16), (1, 16)))
    second_up = normal_values(arg_keys[8], (D, HB), D ** -0.5, 0.0625, ((0, 16), (1, 16)))
    second_down = normal_values(arg_keys[9], (HB, D), HB ** -0.5, 0.078125, ((0, 16), (1, 16)))
    return dict(inputs=inputs, parent_gate=parent_gate, parent_up=parent_up, parent_down=parent_down, first_gate=first_gate, first_up=first_up, first_down=first_down, second_gate=second_gate, second_up=second_up, second_down=second_down)


def matmul(left, right):
    return jnp.dot(left, right, preferred_element_type=jnp.float32)


def inner_rows(left, right):
    return lax.dot_general(left, right, (((0,), (0,)), ((), ())), preferred_element_type=jnp.float32)


def outer_cols(left, right):
    return lax.dot_general(left, right, (((1,), (1,)), ((), ())), preferred_element_type=jnp.float32)


def candidate_pass(inputs, target, gate_w, up_w, down_w):
    pre_gate = matmul(inputs, gate_w)
    pre_up = matmul(inputs, up_w)
    hidden = (jax.nn.silu(pre_gate) * pre_up).astype(jnp.bfloat16)
    output_full = matmul(hidden, down_w)
    error_vals = (output_full - target.astype(jnp.float32)).astype(jnp.bfloat16)
    grad_down = inner_rows(hidden, error_vals).astype(jnp.bfloat16)
    back_grad = outer_cols(error_vals, down_w)
    sigmoid_gate = jax.nn.sigmoid(pre_gate)
    grad_pre_gate = (back_grad * pre_up * sigmoid_gate * (1.0 + pre_gate * (1.0 - sigmoid_gate))).astype(jnp.bfloat16)
    grad_pre_up = (back_grad * pre_gate * sigmoid_gate).astype(jnp.bfloat16)
    grad_gate = inner_rows(inputs, grad_pre_gate).astype(jnp.bfloat16)
    grad_up = inner_rows(inputs, grad_pre_up).astype(jnp.bfloat16)
    return error_vals, grad_gate, grad_up, grad_down


def reference(inputs, parent_gate, parent_up, parent_down, first_gate, first_up, first_down, second_gate, second_up, second_down):
    parent_pre_gate = matmul(inputs, parent_gate)
    parent_pre_up = matmul(inputs, parent_up)
    parent_hidden = (jax.nn.silu(parent_pre_gate) * parent_pre_up).astype(jnp.bfloat16)
    target = matmul(parent_hidden, parent_down).astype(jnp.bfloat16)
    first_error, first_grad_gate, first_grad_up, first_grad_down = candidate_pass(inputs, target, first_gate, first_up, first_down)
    second_error, second_grad_gate, second_grad_up, second_grad_down = candidate_pass(inputs, target, second_gate, second_up, second_down)
    return (target, first_error, second_error, first_grad_gate, first_grad_up, first_grad_down, second_grad_gate, second_grad_up, second_grad_down)
```

```python
import jax
import jax.numpy as jnp
from jax import lax
from jax.sharding import Mesh
from jax.sharding import PartitionSpec as P

BF16 = jnp.bfloat16
F32 = jnp.float32
PAD_A = 512
PAD_B = 384


def shifted(value, axis, step):
    size = lax.axis_size(axis)
    return lax.ppermute(value, axis, [(i, (i - step) % size) for i in range(size)])


def dot(left, right, kind):
    return jnp.dot(left, right, preferred_element_type=F32).astype(kind)


def dot_t(left, right, kind):
    out = lax.dot_general(left, right, (((1,), (1,)), ((), ())), preferred_element_type=F32)
    return out.astype(kind)


def inner_rows(left, right):
    out = lax.dot_general(left, right, (((0,), (0,)), ((), ())), preferred_element_type=F32)
    return out.astype(BF16)


def gather_gw(block):
    pair = jnp.concatenate([block, shifted(block, "grp", 1)], axis=0)
    ring = jnp.concatenate([pair] + [shifted(pair, "x", k) for k in (1, 2, 3)], axis=0)
    return jnp.concatenate([ring, shifted(ring, "core", 1)], axis=0)


def scatter_gw(part):
    half = part.shape[0] // 2
    other = shifted(part[half:].astype(BF16), "core", 1)
    ring = part[:half].astype(F32) + other.astype(F32)
    quarter = half // 4
    total = ring[:quarter]
    for k in (1, 2, 3):
        sent = ring[k * quarter : (k + 1) * quarter].astype(BF16)
        total = total + shifted(sent, "x", -k).astype(F32)
    last = quarter // 2
    return total[:last] + shifted(total[last:].astype(BF16), "grp", 1).astype(F32)


def roll_blocks(rows, y, z):
    cells = rows.reshape(4, 4, -1, rows.shape[1])
    cells = lax.dynamic_slice_in_dim(jnp.concatenate([cells, cells[:3]], axis=0), y, 4, 0)
    cells = lax.dynamic_slice_in_dim(jnp.concatenate([cells, cells[:, :3]], axis=1), z, 4, 1)
    return cells.reshape(rows.shape)


def gather_tok(rows):
    line = jnp.concatenate([rows] + [shifted(rows, "zl", k) for k in (1, 2, 3)], axis=0)
    after = shifted(line, "y", 1)
    before = shifted(line, "y", -1)
    half = line.shape[0] // 2
    far_a = shifted(after[:half], "y", 1)
    far_b = shifted(before[half:], "y", -1)
    return jnp.concatenate([line, after, far_a, far_b, before], axis=0)


def scatter_tok(part_of):
    up = part_of(192, 320, BF16)
    down = part_of(320, 448, BF16)
    up = shifted(up, "y", -1)
    down = shifted(down, "y", 1)
    near = part_of(128, 192, F32)
    near = shifted((near + up[64:].astype(F32)).astype(BF16), "y", -1)
    prev = part_of(448, 512, F32)
    prev = shifted((prev + down[:64].astype(F32)).astype(BF16), "y", 1)
    own = part_of(0, 128, F32)
    top = own[:64] + near.astype(F32) + down[64:].astype(F32)
    low = own[64:] + up[:64].astype(F32) + prev.astype(F32)
    total = top[:32]
    blocks = (top[32:], low[:32], low[32:])
    for k in (1, 2, 3):
        total = total + shifted(blocks[k - 1].astype(BF16), "zl", -k).astype(F32)
    return total


def padded_columns(first, second):
    return jnp.concatenate(
        [
            jnp.pad(first, ((0, 0), (0, PAD_A - first.shape[1]))),
            jnp.pad(second, ((0, 0), (0, PAD_B - second.shape[1]))),
        ],
        axis=1,
    )


def body(
    inputs,
    parent_gate,
    parent_up,
    parent_down,
    first_gate,
    first_up,
    first_down,
    second_gate,
    second_up,
    second_down,
):
    y = lax.axis_index("y")
    z = lax.axis_index("zl")
    width_a = first_gate.shape[1]
    width_b = second_gate.shape[1]
    half = parent_gate.shape[1] // 2
    cand = PAD_A + PAD_B
    weights = [
        jnp.concatenate([parent_gate[:, :half], parent_up[:, :half]], axis=1),
        jnp.concatenate([parent_gate[:, half:], parent_up[:, half:]], axis=1),
        jnp.concatenate(
            [padded_columns(first_gate, second_gate), padded_columns(first_up, second_up)], axis=1
        ),
    ]
    down_a = jnp.pad(first_down, ((0, PAD_A - width_a), (0, 0)))
    down_b = jnp.pad(second_down, ((0, PAD_B - width_b), (0, 0)))

    columns = roll_blocks(gather_gw(inputs), y, z)

    def pre_of(weight):
        return scatter_tok(lambda start, stop, kind: dot(columns[start:stop], weight, kind))

    pre = [pre_of(weight) for weight in weights]

    def hidden_of(both, width):
        gate, up = both[:, :width], both[:, width:]
        return (jax.nn.silu(gate) * up).astype(BF16)

    hidden_p = [gather_tok(hidden_of(pre[i], half)) for i in (0, 1)]
    hidden_c = gather_tok(hidden_of(pre[2], cand))
    back_y, back_z = (4 - y) % 4, (4 - z) % 4

    out_p = dot(hidden_p[0], parent_down[:half], F32) + dot(hidden_p[1], parent_down[half:], F32)
    out_a = dot(hidden_c[:, :PAD_A], down_a, BF16)
    out_b = dot(hidden_c[:, PAD_A:], down_b, BF16)
    out_c = scatter_gw(roll_blocks(jnp.concatenate([out_a, out_b], axis=1), back_y, back_z))
    target = scatter_gw(roll_blocks(out_p.astype(BF16), back_y, back_z)).astype(BF16)

    width = target.shape[1]
    error = (out_c - jnp.concatenate([target, target], axis=1).astype(F32)).astype(BF16)

    gate, up = pre[2][:, :cand], pre[2][:, cand:]
    sig = jax.nn.sigmoid(gate)
    factors = jnp.concatenate([up * sig * (1.0 + gate * (1.0 - sig)), gate * sig], axis=1).astype(BF16)
    factors = gather_tok(factors)

    error_all = roll_blocks(gather_gw(error), y, z)
    error_a, error_b = error_all[:, :width], error_all[:, width:]
    back = scatter_tok(
        lambda start, stop, kind: jnp.concatenate(
            [dot_t(error_a[start:stop], down_a, kind), dot_t(error_b[start:stop], down_b, kind)], axis=1
        )
    )
    grad_down_a = inner_rows(hidden_c[:, :width_a], error_a)
    grad_down_b = inner_rows(hidden_c[:, PAD_A : PAD_A + width_b], error_b)
    back_all = gather_tok(back.astype(BF16)).astype(F32)
    grad_gate = (back_all * factors[:, :cand].astype(F32)).astype(BF16)
    grad_up = (back_all * factors[:, cand:].astype(F32)).astype(BF16)
    return (
        target,
        error[:, :width],
        error[:, width:],
        inner_rows(columns, grad_gate[:, :width_a]),
        inner_rows(columns, grad_up[:, :width_a]),
        grad_down_a,
        inner_rows(columns, grad_gate[:, PAD_A : PAD_A + width_b]),
        inner_rows(columns, grad_up[:, PAD_A : PAD_A + width_b]),
        grad_down_b,
    )


def solution(mesh):
    fine = Mesh(mesh.devices.reshape(2, 4, 4, 4, 2), ("grp", "y", "zl", "x", "core"))
    by_rows = P(("grp", "x", "core"), ("y", "zl"))
    by_columns = P(("y", "zl"), ("grp", "x", "core"))
    layer = (by_columns, by_columns, by_rows)
    return jax.shard_map(
        body,
        mesh=fine,
        in_specs=(by_rows, *layer, *layer, *layer),
        out_specs=(by_rows, by_rows, by_rows, *layer, *layer),
        check_vma=False,
    )
```

```python
import jax
import jax.numpy as jnp
from jax import lax
from jax.experimental.layout import Layout, with_layout_constraint
from jax.sharding import Mesh
from jax.sharding import PartitionSpec as P

BF16 = jnp.bfloat16
F32 = jnp.float32
PAD_A = 512
PAD_B = 384


def shifted(value, axis, step):
    size = lax.axis_size(axis)
    return lax.ppermute(value, axis, [(i, (i - step) % size) for i in range(size)])


def dot(left, right, kind):
    return jnp.dot(left, right, preferred_element_type=F32).astype(kind)


def dot_t(left, right, kind):
    out = lax.dot_general(left, right, (((1,), (1,)), ((), ())), preferred_element_type=F32)
    return out.astype(kind)


def inner_rows(left, right):
    out = lax.dot_general(left, right, (((0,), (0,)), ((), ())), preferred_element_type=F32)
    return out.astype(BF16)


class Order:
    def __init__(self):
        self.last = ()

    def enter(self, *values):
        if not self.last:
            return values
        return lax.optimization_barrier((values, self.last))[0]

    def leave(self, *values):
        self.last = values


def rows_of(blocks):
    return blocks.reshape(-1, blocks.shape[-1])


def gather_x_core(pair):
    ring = jnp.concatenate([pair] + [shifted(pair, "x", k) for k in (1, 2, 3)], axis=0)
    return jnp.concatenate([ring, shifted(ring, "core", 1)], axis=0)


class Reduce:
    def __init__(self, order, part):
        half = part.shape[0] // 2
        self.order = order
        self.part = part[:half]
        order.leave(part)
        self.other = shifted(part[half:], "core", 1)

    def core(self):
        part, other = self.order.enter(self.part, self.other)
        ring = part.astype(F32) + other.astype(F32)
        quarter = ring.shape[0] // 4
        self.total = ring[:quarter]
        sent = [ring[k * quarter : (k + 1) * quarter].astype(BF16) for k in (1, 2, 3)]
        self.order.leave(*sent)
        self.arrived = [shifted(block, "x", -k) for k, block in zip((1, 2, 3), sent)]

    def x(self):
        total, *arrived = self.order.enter(self.total, *self.arrived)
        self.total = total + sum(block.astype(F32) for block in arrived)
        sent = self.total.astype(BF16)
        self.order.leave(sent)
        self.there = shifted(sent, "grp", 1)

    def grp(self):
        total, there = self.order.enter(self.total, self.there)
        return total + jnp.concatenate([there[1:], there[:1]], axis=0).astype(F32)


def roll_z(blocks, z):
    cells = blocks.reshape(4, 4, *blocks.shape[1:])
    cells = lax.dynamic_slice_in_dim(jnp.concatenate([cells, cells[:, :3]], axis=1), z, 4, 1)
    return cells.reshape(blocks.shape)


def roll_y(blocks, y):
    cells = blocks.reshape(4, -1, *blocks.shape[1:])
    cells = lax.dynamic_slice_in_dim(jnp.concatenate([cells, cells[:3]], axis=0), y, 4, 0)
    return cells.reshape(blocks.shape)


def swap_y(cells):
    return lax.all_to_all(cells, "y", split_axis=0, concat_axis=0, tiled=True)


class Scatter:
    def __init__(self, order, left, part_of):
        self.order = order
        self.part_of = part_of
        self.left = left
        left = order.enter(*left)
        first = (part_of(left, 192, 320, BF16), part_of(left, 320, 448, BF16))
        order.leave(*first)
        self.up, self.down = shifted(first[0], "y", -1), shifted(first[1], "y", 1)

    def ring(self):
        left = self.order.enter(*self.left)
        near = self.part_of(left, 128, 192, F32)
        prev = self.part_of(left, 448, 512, F32)
        self.up, self.down, near, prev = self.order.enter(self.up, self.down, near, prev)
        near = (near + self.up[64:].astype(F32)).astype(BF16)
        prev = (prev + self.down[:64].astype(F32)).astype(BF16)
        self.order.leave(near, prev)
        self.near, self.prev = shifted(near, "y", -1), shifted(prev, "y", 1)

    def ring_end(self):
        left = self.order.enter(*self.left)
        own = self.part_of(left, 0, 128, F32)
        near, prev, own = self.order.enter(self.near, self.prev, own)
        top = own[:64] + near.astype(F32) + self.down[64:].astype(F32)
        low = own[64:] + self.up[:64].astype(F32) + prev.astype(F32)
        self.own = top[:32]
        blocks = (top[32:].astype(BF16), low[:32].astype(BF16), low[32:].astype(BF16))
        self.order.leave(*blocks)
        self.arrived = [shifted(block, "zl", -k) for k, block in zip((1, 2, 3), blocks)]

    def line(self):
        own, *arrived = self.order.enter(self.own, *self.arrived)
        return own + sum(block.astype(F32) for block in arrived)


class Gather:
    def __init__(self, order, rows):
        self.order = order
        order.leave(rows)
        self.rows = [rows] + [shifted(rows, "zl", k) for k in (1, 2, 3)]

    def line(self):
        self.four = jnp.concatenate(self.order.enter(*self.rows), axis=0)
        self.order.leave(self.four)
        self.next, self.before = shifted(self.four, "y", 1), shifted(self.four, "y", -1)

    def ring(self):
        self.next, self.before = self.order.enter(self.next, self.before)
        half = self.four.shape[0] // 2
        far = (self.next[:half], self.before[half:])
        self.order.leave(*far)
        self.far = (shifted(far[0], "y", 1), shifted(far[1], "y", -1))

    def ring_end(self):
        far = self.order.enter(*self.far)
        out = jnp.concatenate([self.four, self.next, *far, self.before], axis=0)
        self.order.leave(out)
        return out


def padded_columns(first, second):
    return jnp.concatenate(
        [
            jnp.pad(first, ((0, 0), (0, PAD_A - first.shape[1]))),
            jnp.pad(second, ((0, 0), (0, PAD_B - second.shape[1]))),
        ],
        axis=1,
    )


def body(
    inputs,
    parent_gate,
    parent_up,
    parent_down,
    first_gate,
    first_up,
    first_down,
    second_gate,
    second_up,
    second_down,
):
    y = lax.axis_index("y")
    z = lax.axis_index("zl")
    back_y, back_z = (4 - y) % 4, (4 - z) % 4
    width_a = first_gate.shape[1]
    width_b = second_gate.shape[1]
    cand = PAD_A + PAD_B
    rows = inputs.shape[0]
    weight_c = jnp.concatenate(
        [padded_columns(first_gate, second_gate), padded_columns(first_up, second_up)], axis=1
    )
    down_a = jnp.pad(first_down, ((0, PAD_A - width_a), (0, 0)))
    down_b = jnp.pad(second_down, ((0, PAD_B - width_b), (0, 0)))

    pair = jnp.stack([inputs, shifted(inputs, "grp", 1)])
    columns_z = roll_z(gather_x_core(pair), z)
    columns = rows_of(roll_y(columns_z, y))
    columns_z = rows_of(columns_z)
    order = Order()

    def product(weight):
        return Scatter(order, (columns,), lambda left, start, stop, kind: dot(left[0][start:stop], weight, kind))

    def hidden_of(both):
        width = both.shape[1] // 2
        gate, up = both[:, :width], both[:, width:]
        return (jax.nn.silu(gate) * up).astype(BF16)

    def blocks_of(value):
        return value.reshape(16, 1, rows, -1)

    pre_c = product(weight_c)
    pre_p = product(jnp.concatenate(order.enter(parent_gate, parent_up), axis=1))
    pre_c.ring()
    pre_p.ring()
    pre_c.ring_end()
    both_c = pre_c.line().astype(BF16)
    pre_p.ring_end()
    both_c = Gather(order, both_c)
    both_c.line()
    hidden_p = Gather(order, hidden_of(pre_p.line()))
    both_c.ring()
    hidden_p.line()
    both_c = roll_y(both_c.ring_end(), back_y).astype(F32)
    hidden_c = hidden_of(both_c)
    out_a = dot(hidden_c[:, :PAD_A], down_a, BF16)
    out_b = dot(hidden_c[:, PAD_A:], down_b, BF16)
    out_c = jnp.concatenate([blocks_of(out_a), blocks_of(out_b)], axis=1)
    out_c = Reduce(order, roll_z(out_c, back_z))
    hidden_p.ring()
    out_c.core()
    hidden_p = hidden_p.ring_end()
    out_p = dot(hidden_p, parent_down, F32)
    out_p = roll_z(roll_y(blocks_of(out_p.astype(BF16)), back_y), back_z)
    target = Reduce(order, out_p)
    out_c.x()
    target.core()
    gate, up = order.enter(both_c[:, :cand], both_c[:, cand:])
    sig = jax.nn.sigmoid(gate)
    factor_gate = (up * sig * (1.0 + gate * (1.0 - sig))).astype(BF16)
    factor_up = (gate * sig).astype(BF16)
    order.leave(factor_gate, factor_up)
    target.x()
    out_c = out_c.grp()
    target = target.grp().astype(BF16)
    error = (out_c - target.astype(F32)).astype(BF16)
    error_all = roll_z(gather_x_core(error), z)
    error_a, error_b = rows_of(error_all[:, 0]), rows_of(error_all[:, 1])
    back = jnp.concatenate([dot_t(error_a, down_a, BF16), dot_t(error_b, down_b, BF16)], axis=1)
    back = with_layout_constraint(back, Layout(major_to_minor=(0, 1)))
    back = swap_y(back.reshape(4, -1, cand)).astype(F32).sum(axis=0)
    total = back[:rows]
    for k in (1, 2, 3):
        total = total + shifted(back[k * rows : (k + 1) * rows].astype(BF16), "zl", -k).astype(F32)
    back = total.astype(BF16)
    grad_down_a = inner_rows(hidden_c[:, :width_a], error_a)
    grad_down_b = inner_rows(hidden_c[:, PAD_A : PAD_A + width_b], error_b)
    back = jnp.concatenate([back] + [shifted(back, "zl", k) for k in (1, 2, 3)], axis=0)
    back = swap_y(jnp.broadcast_to(back, (4, *back.shape))).reshape(-1, cand).astype(F32)
    grad_gate = (back * factor_gate.astype(F32)).astype(BF16)
    grad_up = (back * factor_up.astype(F32)).astype(BF16)
    return (
        target[0, 0],
        error[0, 0],
        error[0, 1],
        inner_rows(columns_z, grad_gate[:, :width_a]),
        inner_rows(columns_z, grad_up[:, :width_a]),
        grad_down_a,
        inner_rows(columns_z, grad_gate[:, PAD_A : PAD_A + width_b]),
        inner_rows(columns_z, grad_up[:, PAD_A : PAD_A + width_b]),
        grad_down_b,
    )


def solution(mesh):
    fine = Mesh(mesh.devices.reshape(2, 4, 4, 4, 2), ("grp", "y", "zl", "x", "core"))
    by_rows = P(("grp", "x", "core"), ("y", "zl"))
    by_columns = P(("y", "zl"), ("grp", "x", "core"))
    layer = (by_columns, by_columns, by_rows)
    return jax.shard_map(
        body,
        mesh=fine,
        in_specs=(by_rows, *layer, *layer, *layer),
        out_specs=(by_rows, by_rows, by_rows, *layer, *layer),
        check_vma=False,
    )
```

```python
import jax
import jax.numpy as jnp
from jax import lax
from jax.experimental.layout import Layout, with_layout_constraint
from jax.sharding import Mesh
from jax.sharding import PartitionSpec as P

BF16 = jnp.bfloat16
F32 = jnp.float32
PAD_A = 512
PAD_B = 384


def shifted(value, axis, step):
    size = lax.axis_size(axis)
    return lax.ppermute(value, axis, [(i, (i - step) % size) for i in range(size)])


def dot(left, right, kind):
    return jnp.dot(left, right, preferred_element_type=F32).astype(kind)


def dot_t(left, right, kind):
    out = lax.dot_general(left, right, (((1,), (1,)), ((), ())), preferred_element_type=F32)
    return out.astype(kind)


def inner_rows(left, right):
    out = lax.dot_general(left, right, (((0,), (0,)), ((), ())), preferred_element_type=F32)
    return out.astype(BF16)


class Order:
    def __init__(self):
        self.last = ()

    def enter(self, *values):
        if not self.last:
            return values
        return lax.optimization_barrier((values, self.last))[0]

    def leave(self, *values):
        self.last = values


def rows_of(blocks):
    return blocks.reshape(-1, blocks.shape[-1])


def gather_x_core(pair, *aside):
    ring = jnp.concatenate([pair] + [shifted(pair, "x", k) for k in (1, 2, 3)], axis=0)
    if aside:
        ring, *aside = lax.optimization_barrier((ring, *aside))
        return jnp.concatenate([ring, shifted(ring, "core", 1)], axis=0), *aside
    return jnp.concatenate([ring, shifted(ring, "core", 1)], axis=0)


class Reduce:
    def __init__(self, order, part):
        half = part.shape[0] // 2
        self.order = order
        self.part = part[:half]
        order.leave(part)
        self.other = shifted(part[half:], "core", 1)

    def core(self):
        part, other = self.order.enter(self.part, self.other)
        ring = part.astype(F32) + other.astype(F32)
        quarter = ring.shape[0] // 4
        self.total = ring[:quarter]
        sent = [ring[k * quarter : (k + 1) * quarter].astype(BF16) for k in (1, 2, 3)]
        self.order.leave(*sent)
        self.arrived = [shifted(block, "x", -k) for k, block in zip((1, 2, 3), sent)]

    def x(self):
        total, *arrived = self.order.enter(self.total, *self.arrived)
        self.total = total + sum(block.astype(F32) for block in arrived)
        self.order.leave(self.total)

    def x_end(self):
        (self.total,) = self.order.enter(self.total)
        sent = self.total.astype(BF16)
        self.order.leave(sent)
        self.there = shifted(sent, "grp", 1)

    def grp(self):
        total, there = self.order.enter(self.total, self.there)
        return total + jnp.concatenate([there[1:], there[:1]], axis=0).astype(F32)


def roll_z(blocks, z):
    cells = blocks.reshape(4, 4, *blocks.shape[1:])
    cells = lax.dynamic_slice_in_dim(jnp.concatenate([cells, cells[:, :3]], axis=1), z, 4, 1)
    return cells.reshape(blocks.shape)


def roll_y(blocks, y):
    cells = blocks.reshape(4, -1, *blocks.shape[1:])
    cells = lax.dynamic_slice_in_dim(jnp.concatenate([cells, cells[:3]], axis=0), y, 4, 0)
    return cells.reshape(blocks.shape)


def swap_y(cells):
    return lax.all_to_all(cells, "y", split_axis=0, concat_axis=0, tiled=True)


class Scatter:
    def __init__(self, order, left, part_of):
        self.order = order
        self.part_of = part_of
        self.left = left
        left = order.enter(*left)
        first = (part_of(left, 192, 320, BF16), part_of(left, 320, 448, BF16))
        order.leave(*first)
        self.up, self.down = shifted(first[0], "y", -1), shifted(first[1], "y", 1)

    def ring(self):
        left = self.order.enter(*self.left)
        near = self.part_of(left, 128, 192, F32)
        prev = self.part_of(left, 448, 512, F32)
        self.up, self.down, near, prev = self.order.enter(self.up, self.down, near, prev)
        near = (near + self.up[64:].astype(F32)).astype(BF16)
        prev = (prev + self.down[:64].astype(F32)).astype(BF16)
        self.order.leave(near, prev)
        self.near, self.prev = shifted(near, "y", -1), shifted(prev, "y", 1)

    def ring_end(self):
        left = self.order.enter(*self.left)
        own = self.part_of(left, 0, 128, F32)
        near, prev, own = self.order.enter(self.near, self.prev, own)
        top = own[:64] + near.astype(F32) + self.down[64:].astype(F32)
        low = own[64:] + self.up[:64].astype(F32) + prev.astype(F32)
        self.own = top[:32]
        blocks = (top[32:].astype(BF16), low[:32].astype(BF16), low[32:].astype(BF16))
        self.order.leave(*blocks)
        self.arrived = [shifted(block, "zl", -k) for k, block in zip((1, 2, 3), blocks)]

    def line(self):
        own, *arrived = self.order.enter(self.own, *self.arrived)
        return own + sum(block.astype(F32) for block in arrived)


class Gather:
    def __init__(self, order, rows):
        self.order = order
        order.leave(rows)
        self.rows = [rows] + [shifted(rows, "zl", k) for k in (1, 2, 3)]

    def line(self):
        self.four = jnp.concatenate(self.order.enter(*self.rows), axis=0)
        self.order.leave(self.four)
        self.next, self.before = shifted(self.four, "y", 1), shifted(self.four, "y", -1)

    def ring(self):
        self.next, self.before = self.order.enter(self.next, self.before)
        half = self.four.shape[0] // 2
        far = (self.next[:half], self.before[half:])
        self.order.leave(*far)
        self.far = (shifted(far[0], "y", 1), shifted(far[1], "y", -1))

    def ring_end(self):
        far = self.order.enter(*self.far)
        out = jnp.concatenate([self.four, self.next, *far, self.before], axis=0)
        self.order.leave(out)
        return out


def padded_columns(first, second):
    return jnp.concatenate(
        [
            jnp.pad(first, ((0, 0), (0, PAD_A - first.shape[1]))),
            jnp.pad(second, ((0, 0), (0, PAD_B - second.shape[1]))),
        ],
        axis=1,
    )


def body(
    inputs,
    parent_gate,
    parent_up,
    parent_down,
    first_gate,
    first_up,
    first_down,
    second_gate,
    second_up,
    second_down,
):
    y = lax.axis_index("y")
    z = lax.axis_index("zl")
    back_y, back_z = (4 - y) % 4, (4 - z) % 4
    width_a = first_gate.shape[1]
    width_b = second_gate.shape[1]
    cand = PAD_A + PAD_B
    rows = inputs.shape[0]
    weight_c = jnp.concatenate(
        [padded_columns(first_gate, second_gate), padded_columns(first_up, second_up)], axis=1
    )
    down_a = jnp.pad(first_down, ((0, PAD_A - width_a), (0, 0)))
    down_b = jnp.pad(second_down, ((0, PAD_B - width_b), (0, 0)))

    pair = jnp.stack([inputs, shifted(inputs, "grp", 1)])
    columns, weight_c = gather_x_core(pair, weight_c)
    columns_z = roll_z(columns, z)
    columns = rows_of(roll_y(columns_z, y))
    columns_z = rows_of(columns_z)
    order = Order()

    def product(weight):
        return Scatter(order, (columns,), lambda left, start, stop, kind: dot(left[0][start:stop], weight, kind))

    def hidden_of(both):
        width = both.shape[1] // 2
        gate, up = both[:, :width], both[:, width:]
        return (jax.nn.silu(gate) * up).astype(BF16)

    def blocks_of(value):
        return value.reshape(16, 1, rows, -1)

    pre_c = product(weight_c)
    pre_p = product(jnp.concatenate(order.enter(parent_gate, parent_up), axis=1))
    pre_c.ring()
    pre_p.ring()
    pre_c.ring_end()
    both_c = pre_c.line().astype(BF16)
    pre_p.ring_end()
    both_c = Gather(order, both_c)
    both_c.line()
    hidden_p = Gather(order, hidden_of(pre_p.line()))
    both_c.ring()
    hidden_p.line()
    both_c = roll_y(both_c.ring_end(), back_y).astype(F32)
    hidden_c = hidden_of(both_c)
    out_a = dot(hidden_c[:, :PAD_A], down_a, BF16)
    out_b = dot(hidden_c[:, PAD_A:], down_b, BF16)
    out_c = jnp.concatenate([blocks_of(out_a), blocks_of(out_b)], axis=1)
    out_c = Reduce(order, roll_z(out_c, back_z))
    hidden_p.ring()
    out_c.core()
    hidden_p = hidden_p.ring_end()
    out_p = dot(hidden_p, parent_down, F32)
    out_p = roll_z(roll_y(blocks_of(out_p.astype(BF16)), back_y), back_z)
    target = Reduce(order, out_p)
    out_c.x()
    target.core()
    out_c.x_end()
    gate, up = order.enter(both_c[:, :cand], both_c[:, cand:])
    sig = jax.nn.sigmoid(gate)
    factor_gate = (up * sig * (1.0 + gate * (1.0 - sig))).astype(BF16)
    factor_up = (gate * sig).astype(BF16)
    order.leave(factor_gate, factor_up)
    out_c = out_c.grp()
    order.leave(out_c)
    target.x()
    target.x_end()
    target = target.grp().astype(BF16)
    error = (out_c - target.astype(F32)).astype(BF16)
    error_all = roll_z(gather_x_core(error), z)
    error_a, error_b = rows_of(error_all[:, 0]), rows_of(error_all[:, 1])
    back = jnp.concatenate([dot_t(error_a, down_a, BF16), dot_t(error_b, down_b, BF16)], axis=1)
    back = with_layout_constraint(back, Layout(major_to_minor=(0, 1)))
    back = swap_y(back.reshape(4, -1, cand)).astype(F32).sum(axis=0)
    total = back[:rows]
    for k in (1, 2, 3):
        total = total + shifted(back[k * rows : (k + 1) * rows].astype(BF16), "zl", -k).astype(F32)
    back = total.astype(BF16)
    grad_down_a = inner_rows(hidden_c[:, :width_a], error_a)
    grad_down_b = inner_rows(hidden_c[:, PAD_A : PAD_A + width_b], error_b)
    back = jnp.concatenate([back] + [shifted(back, "zl", k) for k in (1, 2, 3)], axis=0)
    back = lax.all_gather(back, "y", axis=0, tiled=True).astype(F32)
    grad_gate = (back * factor_gate.astype(F32)).astype(BF16)
    grad_up = (back * factor_up.astype(F32)).astype(BF16)
    return (
        target[0, 0],
        error[0, 0],
        error[0, 1],
        inner_rows(columns_z, grad_gate[:, :width_a]),
        inner_rows(columns_z, grad_up[:, :width_a]),
        grad_down_a,
        inner_rows(columns_z, grad_gate[:, PAD_A : PAD_A + width_b]),
        inner_rows(columns_z, grad_up[:, PAD_A : PAD_A + width_b]),
        grad_down_b,
    )


def solution(mesh):
    fine = Mesh(mesh.devices.reshape(2, 4, 4, 4, 2), ("grp", "y", "zl", "x", "core"))
    by_rows = P(("grp", "x", "core"), ("y", "zl"))
    by_columns = P(("y", "zl"), ("grp", "x", "core"))
    layer = (by_columns, by_columns, by_rows)
    return jax.shard_map(
        body,
        mesh=fine,
        in_specs=(by_rows, *layer, *layer, *layer),
        out_specs=(by_rows, by_rows, by_rows, *layer, *layer),
        check_vma=False,
    )
```

```python
import jax
import jax.numpy as jnp
from jax import lax
from jax.experimental.layout import Layout, with_layout_constraint
from jax.sharding import Mesh
from jax.sharding import PartitionSpec as P

BF16 = jnp.bfloat16
F32 = jnp.float32
PAD_A = 512
PAD_B = 384


def shifted(value, axis, step):
    size = lax.axis_size(axis)
    return lax.ppermute(value, axis, [(i, (i - step) % size) for i in range(size)])


def dot(left, right, kind):
    return jnp.dot(left, right, preferred_element_type=F32).astype(kind)


def dot_t(left, right, kind):
    out = lax.dot_general(left, right, (((1,), (1,)), ((), ())), preferred_element_type=F32)
    return out.astype(kind)


def inner_rows(left, right):
    out = lax.dot_general(left, right, (((0,), (0,)), ((), ())), preferred_element_type=F32)
    return out.astype(BF16)


class Order:
    def __init__(self):
        self.last = ()

    def enter(self, *values):
        if not self.last:
            return values
        return lax.optimization_barrier((values, self.last))[0]

    def leave(self, *values):
        self.last = values


def rows_of(blocks):
    return blocks.reshape(-1, blocks.shape[-1])


def gather_x_core(pair, *aside):
    ring = jnp.concatenate([pair] + [shifted(pair, "x", k) for k in (1, 2, 3)], axis=0)
    if aside:
        ring, *aside = lax.optimization_barrier((ring, *aside))
        return jnp.concatenate([ring, shifted(ring, "core", 1)], axis=0), *aside
    return jnp.concatenate([ring, shifted(ring, "core", 1)], axis=0)


class Reduce:
    def __init__(self, order, part):
        half = part.shape[0] // 2
        self.order = order
        self.part = part[:half]
        order.leave(part)
        self.other = shifted(part[half:], "core", 1)

    def core(self):
        part, other = self.order.enter(self.part, self.other)
        ring = part.astype(F32) + other.astype(F32)
        quarter = ring.shape[0] // 4
        self.total = ring[:quarter]
        sent = [ring[k * quarter : (k + 1) * quarter].astype(BF16) for k in (1, 2, 3)]
        self.order.leave(*sent)
        self.arrived = [shifted(block, "x", -k) for k, block in zip((1, 2, 3), sent)]

    def x(self):
        total, *arrived = self.order.enter(self.total, *self.arrived)
        self.total = total + sum(block.astype(F32) for block in arrived)
        self.order.leave(self.total)


def reduce_grp(total):
    there = shifted(total.astype(BF16), "grp", 1).astype(F32)
    return total + jnp.concatenate([there[1:], there[:1]], axis=0)


def roll_z(blocks, z):
    cells = blocks.reshape(4, 4, *blocks.shape[1:])
    cells = lax.dynamic_slice_in_dim(jnp.concatenate([cells, cells[:, :3]], axis=1), z, 4, 1)
    return cells.reshape(blocks.shape)


def roll_y(blocks, y):
    cells = blocks.reshape(4, -1, *blocks.shape[1:])
    cells = lax.dynamic_slice_in_dim(jnp.concatenate([cells, cells[:3]], axis=0), y, 4, 0)
    return cells.reshape(blocks.shape)


def swap_y(cells):
    return lax.all_to_all(cells, "y", split_axis=0, concat_axis=0, tiled=True)


class Scatter:
    def __init__(self, order, left, part_of):
        self.order = order
        self.part_of = part_of
        self.left = left
        left = order.enter(*left)
        first = (part_of(left, 192, 320, BF16), part_of(left, 320, 448, BF16))
        order.leave(*first)
        self.up, self.down = shifted(first[0], "y", -1), shifted(first[1], "y", 1)

    def ring(self):
        left = self.order.enter(*self.left)
        near = self.part_of(left, 128, 192, F32)
        prev = self.part_of(left, 448, 512, F32)
        self.up, self.down, near, prev = self.order.enter(self.up, self.down, near, prev)
        near = (near + self.up[64:].astype(F32)).astype(BF16)
        prev = (prev + self.down[:64].astype(F32)).astype(BF16)
        self.order.leave(near, prev)
        self.near, self.prev = shifted(near, "y", -1), shifted(prev, "y", 1)

    def ring_end(self):
        left = self.order.enter(*self.left)
        own = self.part_of(left, 0, 128, F32)
        near, prev, own = self.order.enter(self.near, self.prev, own)
        top = own[:64] + near.astype(F32) + self.down[64:].astype(F32)
        low = own[64:] + self.up[:64].astype(F32) + prev.astype(F32)
        self.own = top[:32]
        blocks = (top[32:].astype(BF16), low[:32].astype(BF16), low[32:].astype(BF16))
        self.order.leave(*blocks)
        self.arrived = [shifted(block, "zl", -k) for k, block in zip((1, 2, 3), blocks)]

    def line(self):
        own, *arrived = self.order.enter(self.own, *self.arrived)
        return own + sum(block.astype(F32) for block in arrived)


class Gather:
    def __init__(self, order, rows):
        self.order = order
        order.leave(rows)
        self.rows = [rows] + [shifted(rows, "zl", k) for k in (1, 2, 3)]

    def line(self):
        self.four = jnp.concatenate(self.order.enter(*self.rows), axis=0)
        self.order.leave(self.four)
        self.next, self.before = shifted(self.four, "y", 1), shifted(self.four, "y", -1)

    def ring(self):
        self.next, self.before = self.order.enter(self.next, self.before)
        half = self.four.shape[0] // 2
        far = (self.next[:half], self.before[half:])
        self.order.leave(*far)
        self.far = (shifted(far[0], "y", 1), shifted(far[1], "y", -1))

    def ring_end(self):
        far = self.order.enter(*self.far)
        out = jnp.concatenate([self.four, self.next, *far, self.before], axis=0)
        self.order.leave(out)
        return out


def padded_columns(first, second):
    return jnp.concatenate(
        [
            jnp.pad(first, ((0, 0), (0, PAD_A - first.shape[1]))),
            jnp.pad(second, ((0, 0), (0, PAD_B - second.shape[1]))),
        ],
        axis=1,
    )


def body(
    inputs,
    parent_gate,
    parent_up,
    parent_down,
    first_gate,
    first_up,
    first_down,
    second_gate,
    second_up,
    second_down,
):
    y = lax.axis_index("y")
    z = lax.axis_index("zl")
    back_y, back_z = (4 - y) % 4, (4 - z) % 4
    width_a = first_gate.shape[1]
    width_b = second_gate.shape[1]
    cand = PAD_A + PAD_B
    rows = inputs.shape[0]
    weight_c = jnp.concatenate(
        [padded_columns(first_gate, second_gate), padded_columns(first_up, second_up)], axis=1
    )
    down_a = jnp.pad(first_down, ((0, PAD_A - width_a), (0, 0)))
    down_b = jnp.pad(second_down, ((0, PAD_B - width_b), (0, 0)))

    pair = jnp.stack([inputs, shifted(inputs, "grp", 1)])
    columns, weight_c = gather_x_core(pair, weight_c)
    columns_z = roll_z(columns, z)
    columns = rows_of(roll_y(columns_z, y))
    columns_z = rows_of(columns_z)
    order = Order()

    def product(weight):
        return Scatter(order, (columns,), lambda left, start, stop, kind: dot(left[0][start:stop], weight, kind))

    def hidden_of(both):
        width = both.shape[1] // 2
        gate, up = both[:, :width], both[:, width:]
        return (jax.nn.silu(gate) * up).astype(BF16)

    def blocks_of(value):
        return value.reshape(16, 1, rows, -1)

    pre_c = product(weight_c)
    pre_p = product(jnp.concatenate(order.enter(parent_gate, parent_up), axis=1))
    pre_c.ring()
    pre_p.ring()
    pre_c.ring_end()
    both_c = pre_c.line().astype(BF16)
    pre_p.ring_end()
    both_c = Gather(order, both_c)
    both_c.line()
    hidden_p = Gather(order, hidden_of(pre_p.line()))
    both_c.ring()
    hidden_p.line()
    both_c = roll_y(both_c.ring_end(), back_y).astype(F32)
    hidden_c = hidden_of(both_c)
    out_a = dot(hidden_c[:, :PAD_A], down_a, BF16)
    out_b = dot(hidden_c[:, PAD_A:], down_b, BF16)
    out_c = jnp.concatenate([blocks_of(out_a), blocks_of(out_b)], axis=1)
    out_c = Reduce(order, roll_z(out_c, back_z))
    hidden_p.ring()
    out_c.core()
    hidden_p = hidden_p.ring_end()
    out_p = dot(hidden_p, parent_down, F32)
    out_p = roll_z(roll_y(blocks_of(out_p.astype(BF16)), back_y), back_z)
    target = Reduce(order, out_p)
    out_c.x()
    target.core()
    gate, up = order.enter(both_c[:, :cand], both_c[:, cand:])
    sig = jax.nn.sigmoid(gate)
    factor_gate = (up * sig * (1.0 + gate * (1.0 - sig))).astype(BF16)
    factor_up = (gate * sig).astype(BF16)
    order.leave(factor_gate, factor_up)
    target.x()
    outs = reduce_grp(jnp.concatenate([target.total, out_c.total], axis=1))
    target = outs[:, :1].astype(BF16)
    error = (outs[:, 1:] - target.astype(F32)).astype(BF16)
    error_all = roll_z(gather_x_core(error), z)
    error_a, error_b = rows_of(error_all[:, 0]), rows_of(error_all[:, 1])
    back = jnp.concatenate([dot_t(error_a, down_a, BF16), dot_t(error_b, down_b, BF16)], axis=1)
    back = with_layout_constraint(back, Layout(major_to_minor=(0, 1)))
    back = swap_y(back.reshape(4, -1, cand)).astype(F32).sum(axis=0)
    total = back[:rows]
    for k in (1, 2, 3):
        total = total + shifted(back[k * rows : (k + 1) * rows].astype(BF16), "zl", -k).astype(F32)
    back = total.astype(BF16)
    grad_down_a = inner_rows(hidden_c[:, :width_a], error_a)
    grad_down_b = inner_rows(hidden_c[:, PAD_A : PAD_A + width_b], error_b)
    back = jnp.concatenate([back] + [shifted(back, "zl", k) for k in (1, 2, 3)], axis=0)
    back = lax.all_gather(back, "y", axis=0, tiled=True).astype(F32)
    grad_gate = (back * factor_gate.astype(F32)).astype(BF16)
    grad_up = (back * factor_up.astype(F32)).astype(BF16)
    return (
        target[0, 0],
        error[0, 0],
        error[0, 1],
        inner_rows(columns_z, grad_gate[:, :width_a]),
        inner_rows(columns_z, grad_up[:, :width_a]),
        grad_down_a,
        inner_rows(columns_z, grad_gate[:, PAD_A : PAD_A + width_b]),
        inner_rows(columns_z, grad_up[:, PAD_A : PAD_A + width_b]),
        grad_down_b,
    )


def solution(mesh):
    fine = Mesh(mesh.devices.reshape(2, 4, 4, 4, 2), ("grp", "y", "zl", "x", "core"))
    by_rows = P(("grp", "x", "core"), ("y", "zl"))
    by_columns = P(("y", "zl"), ("grp", "x", "core"))
    layer = (by_columns, by_columns, by_rows)
    return jax.shard_map(
        body,
        mesh=fine,
        in_specs=(by_rows, *layer, *layer, *layer),
        out_specs=(by_rows, by_rows, by_rows, *layer, *layer),
        check_vma=False,
    )
```
